256 devices in a mesh: gx: 16 (over y, x_hi, core), gy: 16 (over z, x_lo).
Axes of the slice: x: 4 (x_hi: 2, x_lo: 2; x = x_hi * 2 + x_lo), y: 4, z: 8, core: 2. Of those that a mesh axis runs over, the one named last changes fastest.
Arguments:
- inputs: bfloat16 [256, 16, 48, 512], P(('gx', 'gy')), may hold values from -6 to 6
- grad_out: bfloat16 [256, 16, 48, 512], P(('gx', 'gy')), may hold values from -6 to 6
- conv_kernel: float32 [7, 7, 512], replicated, may hold values from -0.875 to 0.875
- conv_bias: float32 [512], replicated, may hold values from -4 to 4
- layer_norm_gain: float32 [512], replicated, may hold values from 0.1 to 1.9
- layer_norm_bias: float32 [512], replicated, may hold values from -3 to 3
- w_up: bfloat16 [512, 2048], replicated, may hold values from -0.25 to 0.25
- up_bias: float32 [2048], replicated, may hold values from -3 to 3
- w_down: bfloat16 [512, 2048], replicated, may hold values from -0.125 to 0.125
- down_bias: float32 [512], replicated, may hold values from -3 to 3
- layer_scale: float32 [512], replicated, may hold values from 0.1 to 1
Outputs:
- grad_inputs: bfloat16 [256, 16, 48, 512], P(('gx', 'gy'))
- grad_kernel: float32 [7, 7, 512], replicated
- grad_conv_bias: float32 [512], replicated
- grad_ln_gain: float32 [512], replicated
- grad_ln_bias: float32 [512], replicated
- grad_w_up: float32 [512, 2048], replicated
- grad_up_bias: float32 [2048], replicated
- grad_w_down: float32 [512, 2048], replicated
- grad_down_bias: float32 [512], replicated
- grad_layer_scale: float32 [512], replicated
The draws below stay inside these ranges and needn't reach their ends.
All inputs are finite; a program needn't handle non-finite values.
Results may differ from the reference program's by a relative error of at most 0.0063.
Values sent between devices are 32-bit elements; how exact they have to be, the bound alone decides.
No kernel may reach another device: no remote copies, remote signals or barrier semaphores. Data moves between devices by JAX's collectives and lax.ppermute only.
A program may use at most 128 MiB of HBM per device.

```python
import math
import jax
import jax.numpy as jnp
from jax import lax

C = 512
F = 2048
KS = 7
HH = 16
WW = 48
IMAGES = 256


def shard_levels(own_key, extent, pieces, low, high):
    factor_of, own = 1.0, jax.random.fold_in(own_key, 6)
    for axis_at, shards_of in pieces:
        draws = jnp.exp(jax.random.uniform(jax.random.fold_in(own, axis_at), (shards_of,), jnp.float32, low / len(pieces), high / len(pieces)))
        factor_of = factor_of * jnp.repeat(draws, extent[axis_at] // shards_of).reshape([-1 if axis == axis_at else 1 for axis in range(len(extent))])
    return factor_of


def gaussian(rng, shape, spread, reach, split=(), kind=jnp.bfloat16):
    gain = shard_levels(rng, shape, split, -0.22, 0.18) if split else 1.0
    array = jax.random.normal(rng, shape, jnp.float32) * spread * gain
    return jnp.minimum(jnp.maximum(array, -reach), reach).astype(kind)


def setup_inputs(seed: int = 0) -> dict:
    arg_keys = jax.random.split(jax.random.key(seed), 12)
    return {
        "inputs": gaussian(arg_keys[0], (IMAGES, HH, WW, C), 1.0, 6.0, ((0, 256),)),
        "grad_out": gaussian(arg_keys[1], (IMAGES, HH, WW, C), 1.0, 6.0, ((0, 256),)),
        "conv_kernel": gaussian(arg_keys[2], (KS, KS, C), (KS * KS) ** -0.5, 0.875, (), jnp.float32),
        "conv_bias": gaussian(arg_keys[3], (C,), 1.0, 4.0, (), jnp.float32),
        "layer_norm_gain": jnp.clip(1.0 + 0.18 * jax.random.normal(arg_keys[4], (C,), jnp.float32), 0.1, 1.9),
        "layer_norm_bias": gaussian(arg_keys[5], (C,), 0.5, 3.0, (), jnp.float32),
        "w_up": gaussian(arg_keys[6], (C, F), C ** -0.5, 0.25),
        "up_bias": gaussian(arg_keys[7], (F,), 0.5, 3.0, (), jnp.float32),
        "w_down": gaussian(arg_keys[8], (C, F), F ** -0.5, 0.125),
        "down_bias": gaussian(arg_keys[9], (C,), 0.5, 3.0, (), jnp.float32),
        "layer_scale": jnp.clip(jnp.exp(jax.random.uniform(arg_keys[10], (C,), jnp.float32, math.log(0.1), math.log(1.0))), 0.1, 1.0),
    }


def gelu_slope(pre):
    cdf = 0.5 * (1.0 + jax.scipy.special.erf(pre * 0.7071067811865476))
    dens = jnp.exp(-0.5 * pre * pre) * 0.3989422804014327
    return cdf + pre * dens

def one_image(image_in, upstream_in, conv_kernel, conv_bias, layer_norm_gain, layer_norm_bias, w_up, up_bias, w_down, down_bias, layer_scale):
    image = image_in.astype(jnp.float32)
    row_count, column_count, channel_count = image.shape
    padded = jnp.pad(image, ((3, 3), (3, 3), (0, 0)))
    mixed = jnp.zeros_like(image) + conv_bias
    for i in range(KS):
        for j in range(KS):
            mixed = mixed + padded[i:i + row_count, j:j + column_count] * conv_kernel[i, j]
    mean_removed = mixed - lax.optimization_barrier(jnp.mean(mixed, axis=-1, keepdims=True))
    inverse_deviation = lax.rsqrt(lax.optimization_barrier(jnp.mean(mean_removed * mean_removed, axis=-1, keepdims=True)) + 1e-06)
    standardized_input = mean_removed * inverse_deviation
    normalized_output = (standardized_input * layer_norm_gain + layer_norm_bias).astype(jnp.bfloat16).reshape(row_count * column_count, channel_count)
    pre = jnp.dot(normalized_output, w_up, preferred_element_type=jnp.float32) + up_bias
    hidden = jax.nn.gelu(pre, approximate=False).astype(jnp.bfloat16)
    branch = lax.dot_general(hidden, w_down, (((1,), (1,)), ((), ())), preferred_element_type=jnp.float32) + down_bias
    upstream = upstream_in.astype(jnp.float32).reshape(row_count * column_count, channel_count)
    g_scale = lax.optimization_barrier(jnp.sum(upstream * branch, axis=0))
    g_branch = (upstream * layer_scale).astype(jnp.bfloat16)
    gw_down = lax.dot_general(g_branch, hidden, (((0,), (0,)), ((), ())), preferred_element_type=jnp.float32)
    g_down_bias = lax.optimization_barrier(jnp.sum(g_branch.astype(jnp.float32), axis=0))
    g_hidden = jnp.dot(g_branch, w_down, preferred_element_type=jnp.float32)
    g_pre = (g_hidden * gelu_slope(pre)).astype(jnp.bfloat16)
    gw_up = lax.dot_general(normalized_output, g_pre, (((0,), (0,)), ((), ())), preferred_element_type=jnp.float32)
    g_up_bias = lax.optimization_barrier(jnp.sum(g_pre.astype(jnp.float32), axis=0))
    normalized_gradient = lax.dot_general(g_pre, w_up, (((1,), (1,)), ((), ())), preferred_element_type=jnp.float32).reshape(row_count, column_count, channel_count)
    gain_gradient = lax.optimization_barrier(jnp.sum(normalized_gradient * standardized_input, axis=(0, 1)))
    g_lnbias = lax.optimization_barrier(jnp.sum(normalized_gradient, axis=(0, 1)))
    gradient_times_normalized = normalized_gradient * layer_norm_gain
    mixed_gradient = inverse_deviation * (gradient_times_normalized - lax.optimization_barrier(jnp.mean(gradient_times_normalized, axis=-1, keepdims=True)) - standardized_input * lax.optimization_barrier(jnp.mean(gradient_times_normalized * standardized_input, axis=-1, keepdims=True)))
    g_cbias = lax.optimization_barrier(jnp.sum(mixed_gradient, axis=(0, 1)))
    kernel_terms = []
    for i in range(KS):
        for j in range(KS):
            kernel_terms.append(lax.optimization_barrier(jnp.sum(mixed_gradient * padded[i:i + row_count, j:j + column_count], axis=(0, 1))))
    g_kernel = jnp.stack(kernel_terms).reshape(KS, KS, channel_count)
    gpad = jnp.pad(mixed_gradient, ((3, 3), (3, 3), (0, 0)))
    back = upstream_in.astype(jnp.float32)
    for i in range(KS):
        for j in range(KS):
            back = back + gpad[6 - i:6 - i + row_count, 6 - j:6 - j + column_count] * conv_kernel[i, j]
    grads = (g_kernel, g_cbias, gain_gradient, g_lnbias, gw_up, g_up_bias, gw_down, g_down_bias, g_scale)
    return (back.astype(jnp.bfloat16), grads)

def reference(inputs, grad_out, conv_kernel, conv_bias, layer_norm_gain, layer_norm_bias, w_up, up_bias, w_down, down_bias, layer_scale):
    channel_count = inputs.shape[3]
    hid = w_up.shape[1]
    zero_c = jnp.zeros((channel_count,), jnp.float32)
    init = (jnp.zeros((KS, KS, channel_count), jnp.float32), zero_c, zero_c, zero_c, jnp.zeros((channel_count, hid), jnp.float32), jnp.zeros((hid,), jnp.float32), jnp.zeros((channel_count, hid), jnp.float32), zero_c, zero_c)

    def step(carry, pair):
        back, grads = one_image(pair[0], pair[1], conv_kernel, conv_bias, layer_norm_gain, layer_norm_bias, w_up, up_bias, w_down, down_bias, layer_scale)
        return (jax.tree.map(lambda a, b: a + b, carry, grads), back)
    totals, grad_inputs = lax.scan(step, init, (inputs, grad_out))
    means = jax.tree.map(lambda a: a / IMAGES, totals)
    return (grad_inputs, means[0], means[1], means[2], means[3], means[4], means[5], means[6], means[7], means[8])
```

```python
import jax
import jax.numpy as jnp
from jax import lax
from jax.experimental import pallas as pl
from jax.experimental.pallas import tpu as pltpu
from jax.sharding import Mesh
from jax.sharding import PartitionSpec as P


AXES = ("y", "xh", "c", "z", "xl")
XAX = ("xh", "xl")
RING4 = [[(i, (i + s) % 4) for i in range(4)] for s in range(4)]
FLIP = [(0, 1), (1, 0)]


def gelu_slope(pre):
    cdf = 0.5 * (1.0 + jax.scipy.special.erf(pre * 0.7071067811865476))
    dens = jnp.exp(-0.5 * pre * pre) * 0.3989422804014327
    return cdf + pre * dens


def coords():
    x = lax.axis_index("xh") * 2 + lax.axis_index("xl")
    return lax.axis_index("c"), x, lax.axis_index("y")


def relative_rows():
    c, x, y = coords()
    r = lax.iota(jnp.int32, 512)
    far, part, s1, s2, w = r // 256, (r // 128) % 2, (r // 32) % 4, (r // 8) % 4, r % 8
    half = jnp.where(far == 0, 1 - c, c)
    first = jnp.where(part == 0, x, y)
    second = jnp.where(part == 0, y, x)
    return half * 256 + part * 128 + ((first + s1) % 4) * 32 + ((second + s2) % 4) * 8 + w


def scatter_ring(part, axis):
    q = part.shape[0] // 4
    total = part[:q]
    moved = [lax.ppermute(part[s * q : (s + 1) * q], axis, RING4[s]) for s in (1, 2, 3)]
    return total + moved[0] + moved[1] + moved[2]


def gather_ring(piece, axis):
    moved = [lax.ppermute(piece, axis, RING4[s]) for s in (1, 2, 3)]
    return jnp.concatenate([piece] + moved, axis=0)


def reduce_rows(rel):
    width = rel.shape[1]
    mine = rel[256:] + lax.ppermute(rel[:256], "c", FLIP)
    a = scatter_ring(mine[:128], XAX)
    b = scatter_ring(mine[128:], "y")
    a = scatter_ring(a, "y")
    b = scatter_ring(b, XAX)
    ab = jnp.concatenate([a, b], axis=0)
    ab = lax.all_to_all(ab.reshape(16, 8, width // 8).transpose(1, 0, 2), "z", 0, 0, tiled=True)
    piece = jnp.sum(ab, axis=0, keepdims=True)
    full = lax.all_to_all(jnp.broadcast_to(piece, ab.shape), "z", 0, 0, tiled=True)
    ab = full.transpose(1, 0, 2).reshape(16, width)
    a = gather_ring(ab[:8], "y")
    b = gather_ring(ab[8:], XAX)
    a = gather_ring(a, XAX)
    b = gather_ring(b, "y")
    mine = jnp.concatenate([a, b], axis=0)
    return mine, lax.ppermute(mine, "c", FLIP)


def place_kernel(widths, where, mine, other, *rest):
    outs, sem = rest[: len(widths)], rest[-1]
    c, x, y = where[0], where[1], where[2]
    copies = []
    for far, src in ((0, mine), (1, other)):
        for part in range(2):
            for s1 in range(4):
                for s2 in range(4):
                    first, second = (x, y) if part == 0 else (y, x)
                    half = c if far == 0 else 1 - c
                    row = (
                        half * 256
                        + part * 128
                        + lax.rem(first + 4 - s1, 4) * 32
                        + lax.rem(second + 4 - s2, 4) * 8
                    )
                    row = pl.multiple_of(row, 8)
                    at = part * 128 + s1 * 32 + s2 * 8
                    col = 0
                    for o, width in enumerate(widths):
                        copies.append(
                            pltpu.make_async_copy(
                                src.at[pl.ds(at, 8), pl.ds(col, width)],
                                outs[o].at[pl.ds(row, 8), :],
                                sem.at[len(copies)],
                            )
                        )
                        col += width
    for copy in copies:
        copy.start()
    for copy in copies:
        copy.wait()


def place(mine, other, widths):
    c, x, y = coords()
    where = jnp.stack([c, x, y]).astype(jnp.int32)
    vmem = pl.BlockSpec(memory_space=pltpu.VMEM)
    return pl.pallas_call(
        lambda *refs: place_kernel(widths, *refs),
        out_shape=tuple(jax.ShapeDtypeStruct((512, w), jnp.float32) for w in widths),
        in_specs=[pl.BlockSpec(memory_space=pltpu.SMEM), vmem, vmem],
        out_specs=tuple(pl.BlockSpec(memory_space=pl.ANY) for _ in widths),
        scratch_shapes=[pltpu.SemaphoreType.DMA((64 * len(widths),))],
    )(where, mine, other)


def shards(
    inputs,
    grad_out,
    conv_kernel,
    conv_bias,
    layer_norm_gain,
    layer_norm_bias,
    w_up,
    up_bias,
    w_down,
    down_bias,
    layer_scale,
):
    image = inputs[0].astype(jnp.float32)
    row_count, column_count, channel_count = image.shape
    ksize = conv_kernel.shape[0]
    scale = 1.0 / 256
    rows = relative_rows()
    pick = (rows[:, None] == lax.iota(jnp.int32, 512)[None, :])
    pick_bf = pick.astype(jnp.bfloat16)

    padded = jnp.pad(image, ((3, 3), (3, 3), (0, 0)))
    mixed = jnp.zeros_like(image) + conv_bias
    for i in range(ksize):
        for j in range(ksize):
            mixed = mixed + padded[i : i + row_count, j : j + column_count] * conv_kernel[i, j]
    mean_removed = mixed - jnp.mean(mixed, axis=-1, keepdims=True)
    inverse_deviation = lax.rsqrt(
        jnp.mean(mean_removed * mean_removed, axis=-1, keepdims=True) + 1e-06
    )
    standardized_input = mean_removed * inverse_deviation
    normalized_output = (
        (standardized_input * layer_norm_gain + layer_norm_bias)
        .astype(jnp.bfloat16)
        .reshape(row_count * column_count, channel_count)
    )
    pre = jnp.dot(normalized_output, w_up, preferred_element_type=jnp.float32) + up_bias
    hidden = jax.nn.gelu(pre, approximate=False).astype(jnp.bfloat16)
    upstream = grad_out[0].astype(jnp.float32).reshape(row_count * column_count, channel_count)
    g_branch = (upstream * layer_scale).astype(jnp.bfloat16)

    def weight_grad(left, right):
        turned = lax.dot_general(
            pick_bf, left, (((1,), (1,)), ((), ())), preferred_element_type=jnp.bfloat16
        )
        return jnp.dot(turned, right, preferred_element_type=jnp.float32) * scale

    down_rel = weight_grad(g_branch, hidden)
    down_mine, down_other = reduce_rows(down_rel)

    branch = (
        lax.dot_general(
            hidden, w_down, (((1,), (1,)), ((), ())), preferred_element_type=jnp.float32
        )
        + down_bias
    )
    g_scale = jnp.sum(upstream * branch, axis=0)
    g_down_bias = jnp.sum(g_branch.astype(jnp.float32), axis=0)
    g_hidden = jnp.dot(g_branch, w_down, preferred_element_type=jnp.float32)
    g_pre = (g_hidden * gelu_slope(pre)).astype(jnp.bfloat16)
    g_up_bias = jnp.sum(g_pre.astype(jnp.float32), axis=0)
    normalized_gradient = lax.dot_general(
        g_pre, w_up, (((1,), (1,)), ((), ())), preferred_element_type=jnp.float32
    ).reshape(row_count, column_count, channel_count)
    gain_gradient = jnp.sum(normalized_gradient * standardized_input, axis=(0, 1))
    g_lnbias = jnp.sum(normalized_gradient, axis=(0, 1))
    gradient_times_normalized = normalized_gradient * layer_norm_gain
    mixed_gradient = inverse_deviation * (
        gradient_times_normalized
        - jnp.mean(gradient_times_normalized, axis=-1, keepdims=True)
        - standardized_input
        * jnp.mean(gradient_times_normalized * standardized_input, axis=-1, keepdims=True)
    )
    g_cbias = jnp.sum(mixed_gradient, axis=(0, 1))
    kernel_terms = []
    for i in range(ksize):
        for j in range(ksize):
            kernel_terms.append(
                jnp.sum(
                    mixed_gradient * padded[i : i + row_count, j : j + column_count], axis=(0, 1)
                )
            )
    small = jnp.concatenate(
        kernel_terms + [g_cbias, gain_gradient, g_lnbias, g_down_bias, g_scale, g_up_bias]
    )
    small = jnp.pad(small * scale, (0, 65536 - small.shape[0])).reshape(512, 128)
    small_rel = jnp.dot(pick.astype(jnp.float32), small, precision=lax.Precision.HIGHEST)
    up_rel = jnp.concatenate([weight_grad(normalized_output, g_pre), small_rel], axis=1)
    up_mine, up_other = reduce_rows(up_rel)

    gpad = jnp.pad(mixed_gradient, ((3, 3), (3, 3), (0, 0)))
    back = grad_out[0].astype(jnp.float32)
    for i in range(ksize):
        for j in range(ksize):
            back = (
                back
                + gpad[6 - i : 6 - i + row_count, 6 - j : 6 - j + column_count] * conv_kernel[i, j]
            )
    grad_inputs = back.astype(jnp.bfloat16).reshape(1, row_count, column_count, channel_count)

    (gw_down,) = place(down_mine, down_other, (2048,))
    gw_up, small = place(up_mine, up_other, (2048, 128))
    small = small.reshape(-1)
    taps = ksize * ksize * channel_count
    vectors = [small[taps + i * 512 : taps + (i + 1) * 512] for i in range(5)]
    return (
        grad_inputs,
        small[:taps].reshape(ksize, ksize, channel_count),
        vectors[0],
        vectors[1],
        vectors[2],
        gw_up,
        small[taps + 2560 : taps + 4608],
        gw_down,
        vectors[3],
        vectors[4],
    )


def solution(mesh):
    fine = Mesh(mesh.devices.reshape(4, 2, 2, 8, 2), AXES)
    image = P(AXES, None, None, None)
    return jax.shard_map(
        shards,
        mesh=fine,
        in_specs=(image, image) + (P(),) * 9,
        out_specs=(image,) + (P(),) * 9,
        check_vma=False,
    )
```

```python
import jax
import jax.numpy as jnp
from jax import lax
from jax.experimental import pallas as pl
from jax.experimental.pallas import tpu as pltpu
from jax.sharding import Mesh
from jax.sharding import PartitionSpec as P


AXES = ("y", "xh", "c", "z", "xl")
XAX = ("xh", "xl")
PLANE = ("y", "xh", "xl")
RING4 = [[(i, (i + s) % 4) for i in range(4)] for s in range(4)]
FLIP = [(0, 1), (1, 0)]


def gelu_slope(pre):
    cdf = 0.5 * (1.0 + jax.scipy.special.erf(pre * 0.7071067811865476))
    dens = jnp.exp(-0.5 * pre * pre) * 0.3989422804014327
    return cdf + pre * dens


def coords():
    x = lax.axis_index("xh") * 2 + lax.axis_index("xl")
    return lax.axis_index("c"), x, lax.axis_index("y")


def after(value, *others):
    return lax.optimization_barrier((value,) + others)[0]


def own_half_last(channels):
    c = lax.axis_index("c")
    low, high = channels[:, :256], channels[:, 256:]
    return jnp.where(c == 0, high, low), jnp.where(c == 0, low, high)


def contract(left, right):
    return lax.dot_general(
        left, right, (((0,), (0,)), ((), ())), preferred_element_type=jnp.float32
    )


def scatter_plane(mine):
    width = mine.shape[1]
    moved = lax.all_to_all(mine.reshape(16, 16, width), PLANE, 0, 0, tiled=True)
    return jnp.sum(moved, axis=0)


def over_z(piece):
    width = piece.shape[1]
    moved = lax.all_to_all(piece.reshape(8, 2, width), "z", 0, 0, tiled=True)
    summed = jnp.sum(moved, axis=0, keepdims=True)
    full = lax.all_to_all(jnp.broadcast_to(summed, moved.shape), "z", 0, 0, tiled=True)
    return full.reshape(16, width)


def gather_near(piece, axis):
    return jnp.concatenate(
        [piece] + [lax.ppermute(piece, axis, RING4[s]) for s in (1, 2, 3)], axis=0
    )


def gather_plane(piece):
    parts = ((gather_near(piece[:8], "y"), XAX), (gather_near(piece[8:], XAX), "y"))
    first = [(lax.ppermute(p, ax, RING4[1]), lax.ppermute(p, ax, RING4[3])) for p, ax in parts]
    out = []
    for (p, ax), (below, above) in zip(parts, first):
        far = (lax.ppermute(below[:16], ax, RING4[1]), lax.ppermute(above[16:], ax, RING4[3]))
        out += [p, below, above, far[0], far[1]]
    return out + [lax.ppermute(p, "c", FLIP) for p in out]


def place_kernel(where, *refs):
    pieces, outs, sem = refs[:20], refs[20:23], refs[23]
    c, x, y = where[0], where[1], where[2]
    copies = []
    for far in range(2):
        half = c if far == 0 else 1 - c
        for part in range(2):
            first, second = (x, y) if part == 0 else (y, x)
            for k, (s1, low, count) in enumerate(
                ((0, 0, 4), (1, 0, 4), (3, 0, 4), (2, 0, 2), (2, 2, 2))
            ):
                p1 = lax.rem(first + 4 - s1, 4)
                for s2 in range(low, low + count):
                    p2 = lax.rem(second + 4 - s2, 4)
                    at = p2 * 4 + p1 if part == 0 else p1 * 4 + p2
                    row = pl.multiple_of(half * 256 + at * 16 + part * 8, 8)
                    src = pieces[far * 10 + part * 5 + k]
                    for o, (col, width) in zip(outs, ((0, 2048), (2048, 2048), (4096, 128))):
                        copies.append(
                            pltpu.make_async_copy(
                                src.at[pl.ds((s2 - low) * 8, 8), pl.ds(col, width)],
                                o.at[pl.ds(row, 8), :],
                                sem.at[len(copies)],
                            )
                        )
    for copy in copies:
        copy.start()
    for copy in copies:
        copy.wait()


def place(pieces):
    c, x, y = coords()
    where = jnp.stack([c, x, y]).astype(jnp.int32)
    vmem = pl.BlockSpec(memory_space=pltpu.VMEM)
    return pl.pallas_call(
        place_kernel,
        out_shape=tuple(jax.ShapeDtypeStruct((512, w), jnp.float32) for w in (2048, 2048, 128)),
        in_specs=[pl.BlockSpec(memory_space=pltpu.SMEM)] + [vmem] * 20,
        out_specs=(pl.BlockSpec(memory_space=pl.ANY),) * 3,
        scratch_shapes=[pltpu.SemaphoreType.DMA((192,))],
    )(where, *pieces)


def forward_kernel(image, kernel, bias, gain, shift, xhat, normed, inv, pad):
    pad[...] = jnp.zeros_like(pad)

    @pl.loop(0, 16)
    def _(h):
        for b in range(4):
            pad[b, h + 3, pl.ds(8, 48), :] = image[h, :, b * 128 : b * 128 + 128].astype(
                jnp.float32
            )

    @pl.loop(0, 16)
    def _(h):
        mixed = []
        for b in range(4):
            lanes = slice(b * 128, b * 128 + 128)
            acc = jnp.broadcast_to(bias[:, lanes], (48, 128))
            for i in range(7):
                for j in range(7):
                    t = i * 7 + j
                    acc = acc + pad[b, h + i, pl.ds(5 + j, 48), :] * kernel[t : t + 1, lanes]
            mixed.append(acc)
        total = mixed[0] + mixed[1] + mixed[2] + mixed[3]
        mean = jnp.sum(total, axis=-1, keepdims=True) * (1.0 / 512)
        mixed = [m - mean for m in mixed]
        square = mixed[0] * mixed[0]
        for m in mixed[1:]:
            square = square + m * m
        rest = lax.rsqrt(jnp.sum(square, axis=-1, keepdims=True) * (1.0 / 512) + 1e-06)
        rows = pl.ds(pl.multiple_of(h * 48, 48), 48)
        inv[rows, :] = rest
        for b in range(4):
            lanes = slice(b * 128, b * 128 + 128)
            unit = mixed[b] * rest
            xhat[rows, lanes] = unit
            normed[rows, lanes] = (unit * gain[:, lanes] + shift[:, lanes]).astype(jnp.bfloat16)


def forward(image, kernel, bias, gain, shift):
    return pl.pallas_call(
        forward_kernel,
        out_shape=(
            jax.ShapeDtypeStruct((768, 512), jnp.float32),
            jax.ShapeDtypeStruct((768, 512), jnp.bfloat16),
            jax.ShapeDtypeStruct((768, 1), jnp.float32),
        ),
        scratch_shapes=[pltpu.VMEM((4, 22, 64, 128), jnp.float32)],
        compiler_params=pltpu.CompilerParams(vmem_limit_bytes=40 << 20),
        name="conv_norm",
    )(image, kernel, bias, gain, shift)


def backward_kernel(gn, xhat, inv, gain, image, upstream, kernel, out, taps, sums, pad, acc):
    pad[...] = jnp.zeros_like(pad)
    sums[...] = jnp.zeros_like(sums)

    def fold(v):
        return jnp.sum(v.reshape(6, 8, 128), axis=0)

    @pl.loop(0, 16)
    def _(h):
        rows = pl.ds(pl.multiple_of(h * 48, 48), 48)
        rest = inv[rows, :]
        gx, xs = [], []
        for b in range(4):
            lanes = slice(b * 128, b * 128 + 128)
            g, x = gn[rows, lanes], xhat[rows, lanes]
            sums[0, :, lanes] += fold(g * x)
            sums[1, :, lanes] += fold(g)
            gx.append(g * gain[:, lanes])
            xs.append(x)
        plain = gx[0] + gx[1] + gx[2] + gx[3]
        cross = gx[0] * xs[0] + gx[1] * xs[1] + gx[2] * xs[2] + gx[3] * xs[3]
        m1 = jnp.sum(plain, axis=-1, keepdims=True) * (1.0 / 512)
        m2 = jnp.sum(cross, axis=-1, keepdims=True) * (1.0 / 512)
        for b in range(4):
            gm = rest * (gx[b] - m1 - xs[b] * m2)
            sums[2, :, b * 128 : b * 128 + 128] += fold(gm)
            pad[b, h + 3, pl.ds(8, 48), :] = gm

    for b in range(4):
        lanes = slice(b * 128, b * 128 + 128)
        acc[...] = jnp.zeros_like(acc)

        @pl.loop(0, 16)
        def _(h):
            x = image[h, :, lanes].astype(jnp.float32)
            back = upstream[h, :, lanes].astype(jnp.float32)
            for i in range(7):
                for j in range(7):
                    t = i * 7 + j
                    g = pad[b, h + 6 - i, pl.ds(11 - j, 48), :]
                    back = back + g * kernel[t : t + 1, lanes]
                    acc[t] += fold(g * x)
            out[h, :, lanes] = back.astype(jnp.bfloat16)

        for t in range(49):
            taps[t : t + 1, lanes] = jnp.sum(acc[t], axis=0, keepdims=True)


def backward(gn, xhat, inv, gain, image, upstream, kernel):
    return pl.pallas_call(
        backward_kernel,
        out_shape=(
            jax.ShapeDtypeStruct((16, 48, 512), jnp.bfloat16),
            jax.ShapeDtypeStruct((49, 512), jnp.float32),
            jax.ShapeDtypeStruct((3, 8, 512), jnp.float32),
        ),
        scratch_shapes=[
            pltpu.VMEM((4, 22, 64, 128), jnp.float32),
            pltpu.VMEM((49, 8, 128), jnp.float32),
        ],
        compiler_params=pltpu.CompilerParams(vmem_limit_bytes=40 << 20),
        cost_estimate=pl.CostEstimate(flops=80000000, bytes_accessed=6000000, transcendentals=0),
        name="conv_back",
    )(gn, xhat, inv, gain, image, upstream, kernel)


def shards(
    inputs,
    grad_out,
    conv_kernel,
    conv_bias,
    layer_norm_gain,
    layer_norm_bias,
    w_up,
    up_bias,
    w_down,
    down_bias,
    layer_scale,
):
    image = inputs[0]
    row_count, column_count, channel_count = image.shape
    ksize = conv_kernel.shape[0]
    scale = 1.0 / 256
    taps_in = conv_kernel.reshape(49, 512)
    gain_row = layer_norm_gain.reshape(1, 512)
    standardized_input, normalized_output, inverse_deviation = forward(
        image, taps_in, conv_bias.reshape(1, 512), gain_row, layer_norm_bias.reshape(1, 512)
    )
    pre = jnp.dot(normalized_output, w_up, preferred_element_type=jnp.float32) + up_bias
    hidden = jax.nn.gelu(pre, approximate=False).astype(jnp.bfloat16)
    upstream = grad_out[0].astype(jnp.float32).reshape(row_count * column_count, channel_count)
    g_branch = (upstream * layer_scale).astype(jnp.bfloat16)

    gb_send, gb_keep = own_half_last(g_branch)
    down_send = contract(gb_send, hidden) * scale
    down_keep = contract(gb_keep, hidden) * scale
    down_mine = down_keep + lax.ppermute(down_send, "c", FLIP)

    g_branch_b, pre, _ = lax.optimization_barrier((g_branch, pre, down_send))
    g_hidden = jnp.dot(g_branch_b, w_down, preferred_element_type=jnp.float32)
    g_pre = (g_hidden * gelu_slope(pre)).astype(jnp.bfloat16)

    g_pre, down_mine = lax.optimization_barrier((g_pre, down_mine))
    down_piece = scatter_plane(down_mine)
    norm_send, norm_keep = own_half_last(normalized_output)
    up_send = contract(norm_send, g_pre) * scale
    up_keep = contract(norm_keep, g_pre) * scale
    up_recv = lax.ppermute(up_send, "c", FLIP)

    g_pre_b = after(g_pre, up_keep)
    normalized_gradient = lax.dot_general(
        g_pre_b, w_up, (((1,), (1,)), ((), ())), preferred_element_type=jnp.float32
    )
    grad_inputs, g_kernel, sums = backward(
        normalized_gradient,
        standardized_input,
        inverse_deviation,
        gain_row,
        image,
        grad_out[0],
        taps_in,
    )
    gain_gradient, g_lnbias, g_cbias = jnp.sum(sums, axis=1)
    grad_inputs = grad_inputs.reshape(1, row_count, column_count, channel_count)

    g_up_bias = jnp.sum(g_pre_b.astype(jnp.float32), axis=0)
    branch = (
        lax.dot_general(
            hidden, w_down, (((1,), (1,)), ((), ())), preferred_element_type=jnp.float32
        )
        + down_bias
    )
    g_scale = jnp.sum(upstream * branch, axis=0)
    g_down_bias = jnp.sum(g_branch.astype(jnp.float32), axis=0)
    small = jnp.concatenate(
        [g_kernel.reshape(-1), g_cbias, gain_gradient, g_lnbias, g_down_bias, g_scale, g_up_bias]
    )
    small = jnp.pad(small * scale, (0, 65536 - small.shape[0])).reshape(512, 128)
    c = lax.axis_index("c")
    small_send = jnp.where(c == 0, small[256:], small[:256])
    small_keep = jnp.where(c == 0, small[:256], small[256:])
    small_mine = small_keep + lax.ppermute(small_send, "c", FLIP)
    up_mine = jnp.concatenate([up_keep + up_recv, small_mine], axis=1)
    up_mine, down_piece = lax.optimization_barrier((up_mine, down_piece))
    up_piece = scatter_plane(up_mine)

    piece = over_z(jnp.concatenate([down_piece, up_piece], axis=1))
    gw_down, gw_up, small = place(gather_plane(piece))
    small = small.reshape(-1)
    taps = ksize * ksize * channel_count
    vectors = [small[taps + i * 512 : taps + (i + 1) * 512] for i in range(5)]
    return (
        grad_inputs,
        small[:taps].reshape(ksize, ksize, channel_count),
        vectors[0],
        vectors[1],
        vectors[2],
        gw_up,
        small[taps + 2560 : taps + 4608],
        gw_down,
        vectors[3],
        vectors[4],
    )


def solution(mesh):
    fine = Mesh(mesh.devices.reshape(4, 2, 2, 8, 2), AXES)
    image = P(AXES, None, None, None)
    return jax.shard_map(
        shards,
        mesh=fine,
        in_specs=(image, image) + (P(),) * 9,
        out_specs=(image,) + (P(),) * 9,
        check_vma=False,
    )
```

```python
import jax
import jax.numpy as jnp
from jax import lax
from jax.experimental import pallas as pl
from jax.experimental.pallas import tpu as pltpu
from jax.sharding import Mesh
from jax.sharding import PartitionSpec as P


AXES = ("y", "xh", "c", "z", "xl")
XAX = ("xh", "xl")
PLANE = ("y", "xh", "xl")
RING4 = [[(i, (i + s) % 4) for i in range(4)] for s in range(4)]
FLIP = [(0, 1), (1, 0)]


def gelu_cdf(pre):
    return 0.5 * (1.0 + lax.erf(pre * 0.7071067811865476))


def gelu_slope(pre):
    cdf = gelu_cdf(pre)
    dens = jnp.exp(-0.5 * pre * pre) * 0.3989422804014327
    return cdf + pre * dens


def coords():
    x = lax.axis_index("xh") * 2 + lax.axis_index("xl")
    return lax.axis_index("c"), x, lax.axis_index("y")


def after(value, *others):
    return lax.optimization_barrier((value,) + others)[0]


def own_half_last(channels):
    c = lax.axis_index("c")
    low, high = channels[:, :256], channels[:, 256:]
    return jnp.where(c == 0, high, low), jnp.where(c == 0, low, high)


def contract(left, right):
    return lax.dot_general(
        left, right, (((0,), (0,)), ((), ())), preferred_element_type=jnp.float32
    )


def scatter_z(piece):
    width = piece.shape[1]
    moved = lax.all_to_all(piece.reshape(8, 2, width), "z", 0, 0, tiled=True)
    return jnp.sum(moved, axis=0, keepdims=True)


def gather_z(summed):
    width = summed.shape[2]
    full = lax.all_to_all(jnp.broadcast_to(summed, (8, 2, width)), "z", 0, 0, tiled=True)
    return full.reshape(16, width)


def double_z(piece):
    for step in (1, 2, 4):
        piece = piece + lax.ppermute(piece, "z", [(i, i ^ step) for i in range(8)])
    return piece


def gather_near(piece):
    return [
        jnp.concatenate([p] + [lax.ppermute(p, ax, RING4[s]) for s in (1, 2, 3)], axis=0)
        for p, ax in ((piece[:8], "y"), (piece[8:], XAX))
    ]


def gather_sides(near):
    return [
        (lax.ppermute(p, ax, RING4[1]), lax.ppermute(p, ax, RING4[3]))
        for p, ax in zip(near, (XAX, "y"))
    ]


def gather_rest(near, sides):
    out = []
    for p, (below, above), ax in zip(near, sides, (XAX, "y")):
        far = (lax.ppermute(below[:16], ax, RING4[1]), lax.ppermute(above[16:], ax, RING4[3]))
        out += [p, below, above, far[0], far[1]]
    return out, [lax.ppermute(p, "c", FLIP) for p in out]


def place_kernel(far, where, *refs):
    pieces, outs, sem = refs[:10], refs[-4:-1], refs[-1]
    core, x, y = where[0], where[1], where[2]
    half = core if far == 0 else 1 - core
    copies = []

    def copy(src, dst):
        copies.append(pltpu.make_async_copy(src, dst, sem.at[len(copies)]))

    for part in range(2):
        first, second = (x, y) if part == 0 else (y, x)
        for k, (s1, low, count) in enumerate(
            ((0, 0, 4), (1, 0, 4), (3, 0, 4), (2, 0, 2), (2, 2, 2))
        ):
            p1 = lax.rem(first + 4 - s1, 4)
            for s2 in range(low, low + count):
                p2 = lax.rem(second + 4 - s2, 4)
                at = p2 * 4 + p1 if part == 0 else p1 * 4 + p2
                src = pieces[part * 5 + k].at[pl.ds((s2 - low) * 8, 8), :]
                row = pl.multiple_of(half * 256 + at * 16 + part * 8, 8)
                copy(src.at[:, pl.ds(0, 2048)], outs[0].at[pl.ds(row, 8), :])
                copy(src.at[:, pl.ds(2048, 2048)], outs[1].at[pl.ds(row, 8), :])
                if part == 0:
                    row = pl.multiple_of(half * 32 + p1 * 8, 8)
                    lane = pl.multiple_of(p2 * 128, 128)
                    copy(
                        src.at[:, pl.ds(4096, 128)],
                        outs[2].at[pl.ds(row, 8), pl.ds(lane, 128)],
                    )
    for c in copies:
        c.start()
    for c in copies:
        c.wait()


def place(own, other):
    c, x, y = coords()
    where = jnp.stack([c, x, y]).astype(jnp.int32)
    vmem = pl.BlockSpec(memory_space=pltpu.VMEM)
    anywhere = pl.BlockSpec(memory_space=pl.ANY)
    shapes = tuple(
        jax.ShapeDtypeStruct(sh, jnp.float32) for sh in ((512, 2048), (512, 2048), (64, 512))
    )

    def call(far, pieces, whole):
        return pl.pallas_call(
            lambda *refs: place_kernel(far, *refs),
            out_shape=shapes,
            in_specs=[pl.BlockSpec(memory_space=pltpu.SMEM)] + [vmem] * 10 + [anywhere] * len(whole),
            out_specs=(anywhere,) * 3,
            scratch_shapes=[pltpu.SemaphoreType.DMA((80,))],
            input_output_aliases={11 + i: i for i in range(len(whole))},
        )(where, *pieces, *whole)

    return call(1, other, call(0, own, ()))


def forward_kernel(image, kernel, bias, gain, shift, xhat, normed, inv, pad):
    pad[...] = jnp.zeros_like(pad)

    @pl.loop(0, 16)
    def _(h):
        for b in range(4):
            pad[b, h + 3, pl.ds(8, 48), :] = image[h, :, b * 128 : b * 128 + 128].astype(
                jnp.float32
            )

    for b in range(4):
        lanes = slice(b * 128, b * 128 + 128)

        @pl.loop(0, 4)
        def _(group):
            h = group * 4
            acc = [jnp.broadcast_to(bias[:, lanes], (48, 128))] * 4
            for r in range(10):
                for j in range(7):
                    v = pad[b, h + r, pl.ds(5 + j, 48), :]
                    for k in range(4):
                        if 0 <= r - k < 7:
                            acc[k] = acc[k] + v * kernel[r - k, j : j + 1, lanes]
            for k in range(4):
                xhat[pl.ds(pl.multiple_of((h + k) * 48, 48), 48), lanes] = acc[k]

    @pl.loop(0, 16)
    def _(h):
        rows = pl.ds(pl.multiple_of(h * 48, 48), 48)
        mixed = xhat[rows, :]
        mixed = mixed - jnp.mean(mixed, axis=-1, keepdims=True)
        rest = lax.rsqrt(jnp.mean(mixed * mixed, axis=-1, keepdims=True) + 1e-06)
        inv[rows, :] = rest
        unit = mixed * rest
        xhat[rows, :] = unit
        normed[rows, :] = (unit * gain[...] + shift[...]).astype(jnp.bfloat16)


def forward(image, kernel, bias, gain, shift):
    return pl.pallas_call(
        forward_kernel,
        out_shape=(
            jax.ShapeDtypeStruct((768, 512), jnp.float32),
            jax.ShapeDtypeStruct((768, 512), jnp.bfloat16),
            jax.ShapeDtypeStruct((768, 1), jnp.float32),
        ),
        scratch_shapes=[pltpu.VMEM((4, 22, 64, 128), jnp.float32)],
        compiler_params=pltpu.CompilerParams(vmem_limit_bytes=40 << 20),
        name="conv_norm",
    )(image, kernel, bias, gain, shift)


def backward_kernel(gn, xhat, inv, gain, image, upstream, kernel, out, taps, pad, sums, acc):
    pad[...] = jnp.zeros_like(pad)
    sums[...] = jnp.zeros_like(sums)

    def fold(v):
        return jnp.sum(v.reshape(6, 8, 128), axis=0)

    @pl.loop(0, 16)
    def _(h):
        rows = pl.ds(pl.multiple_of(h * 48, 48), 48)
        rest = inv[rows, :]
        gx, xs = [], []
        for b in range(4):
            lanes = slice(b * 128, b * 128 + 128)
            g, x = gn[rows, lanes], xhat[rows, lanes]
            sums[0, :, lanes] += fold(g * x)
            sums[1, :, lanes] += fold(g)
            gx.append(g * gain[:, lanes])
            xs.append(x)
        plain = gx[0] + gx[1] + gx[2] + gx[3]
        cross = gx[0] * xs[0] + gx[1] * xs[1] + gx[2] * xs[2] + gx[3] * xs[3]
        m1 = jnp.sum(plain, axis=-1, keepdims=True) * (1.0 / 512)
        m2 = jnp.sum(cross, axis=-1, keepdims=True) * (1.0 / 512)
        for b in range(4):
            gm = rest * (gx[b] - m1 - xs[b] * m2)
            sums[2, :, b * 128 : b * 128 + 128] += fold(gm)
            pad[b, h + 3, pl.ds(8, 48), :] = gm

    for b in range(4):
        lanes = slice(b * 128, b * 128 + 128)
        acc[...] = jnp.zeros_like(acc)

        @pl.loop(0, 16)
        def _(h):
            x = image[h, :, lanes].astype(jnp.float32)
            back = upstream[h, :, lanes].astype(jnp.float32)
            for i in range(7):
                for j in range(7):
                    t = i * 7 + j
                    g = pad[b, h + 6 - i, pl.ds(11 - j, 48), :]
                    back = back + g * kernel[i, j : j + 1, lanes]
                    acc[t] += fold(g * x)
            out[h, :, lanes] = back.astype(jnp.bfloat16)

        for t in range(49):
            taps[t : t + 1, lanes] = jnp.sum(acc[t], axis=0, keepdims=True) * (1.0 / 256)

    for t in range(3):
        taps[49 + t : 50 + t, :] = jnp.sum(sums[t], axis=0, keepdims=True) * (1.0 / 256)


def backward(gn, xhat, inv, gain, image, upstream, kernel):
    return pl.pallas_call(
        backward_kernel,
        out_shape=(
            jax.ShapeDtypeStruct((16, 48, 512), jnp.bfloat16),
            jax.ShapeDtypeStruct((52, 512), jnp.float32),
        ),
        scratch_shapes=[
            pltpu.VMEM((4, 22, 64, 128), jnp.float32),
            pltpu.VMEM((3, 8, 512), jnp.float32),
            pltpu.VMEM((49, 8, 128), jnp.float32),
        ],
        compiler_params=pltpu.CompilerParams(vmem_limit_bytes=40 << 20),
        cost_estimate=pl.CostEstimate(flops=80000000, bytes_accessed=6000000, transcendentals=0),
        name="conv_back",
    )(gn, xhat, inv, gain, image, upstream, kernel)


def body(
    inputs,
    grad_out,
    conv_kernel,
    conv_bias,
    layer_norm_gain,
    layer_norm_bias,
    w_up,
    up_bias,
    w_down,
    down_bias,
    layer_scale,
):
    image = inputs[0]
    row_count, column_count, channel_count = image.shape
    ksize = conv_kernel.shape[0]
    scale = 1.0 / 256
    gain_row = layer_norm_gain.reshape(1, 512)
    standardized_input, normalized_output, inverse_deviation = forward(
        image, conv_kernel, conv_bias.reshape(1, 512), gain_row, layer_norm_bias.reshape(1, 512)
    )
    pre = jnp.dot(normalized_output, w_up, preferred_element_type=jnp.float32) + up_bias
    hidden = (pre * gelu_cdf(pre)).astype(jnp.bfloat16)
    upstream = grad_out[0].astype(jnp.float32).reshape(row_count * column_count, channel_count)
    g_branch = (upstream * layer_scale).astype(jnp.bfloat16)

    gb_send, gb_keep = own_half_last(g_branch)
    down_send = contract(gb_send, hidden) * scale
    down_keep = contract(gb_keep, hidden) * scale
    down_mine = down_keep + lax.ppermute(down_send, "c", FLIP)

    g_branch_b, pre, _ = lax.optimization_barrier((g_branch, pre, down_send))
    g_hidden = jnp.dot(g_branch_b, w_down, preferred_element_type=jnp.float32)
    g_pre = (g_hidden * gelu_slope(pre)).astype(jnp.bfloat16)

    g_pre, down_mine = lax.optimization_barrier((g_pre, down_mine))
    moved = lax.all_to_all(down_mine.reshape(16, 16, 2048), PLANE, 0, 0, tiled=True)
    norm_send, norm_keep = own_half_last(normalized_output)
    up_send = contract(norm_send, g_pre) * scale
    up_keep = contract(norm_keep, g_pre) * scale
    up_recv = lax.ppermute(up_send, "c", FLIP)

    g_pre_b = after(g_pre, up_keep)
    normalized_gradient = lax.dot_general(
        g_pre_b, w_up, (((1,), (1,)), ((), ())), preferred_element_type=jnp.float32
    )
    grad_inputs, block = backward(
        normalized_gradient,
        standardized_input,
        inverse_deviation,
        gain_row,
        image,
        grad_out[0],
        conv_kernel,
    )
    grad_inputs = grad_inputs.reshape(1, row_count, column_count, channel_count)

    hidden_b, g_pre_c, upstream, _ = lax.optimization_barrier((hidden, g_pre, upstream, up_keep))
    g_up_bias = jnp.sum(g_pre_c.astype(jnp.float32), axis=0)
    branch = (
        lax.dot_general(
            hidden_b, w_down, (((1,), (1,)), ((), ())), preferred_element_type=jnp.float32
        )
        + down_bias
    )
    g_scale = jnp.sum(upstream * branch, axis=0)
    g_down_bias = jnp.sum((upstream * layer_scale).astype(jnp.bfloat16).astype(jnp.float32), axis=0)
    rows = jnp.concatenate([g_down_bias, g_scale, g_up_bias]).reshape(6, 512) * scale
    block = jnp.concatenate([block, rows, jnp.zeros((6, 512), jnp.float32)], axis=0)
    c = lax.axis_index("c")
    small_send = jnp.where(c == 0, block[32:], block[:32])
    small_keep = jnp.where(c == 0, block[:32], block[32:])
    small_mine = small_keep + lax.ppermute(small_send, "c", FLIP)
    small_mine = small_mine.reshape(4, 8, 4, 128).transpose(2, 0, 1, 3).reshape(16, 8, 128)
    small_mine = jnp.pad(small_mine, ((0, 0), (0, 8), (0, 0)))
    up_mine = jnp.concatenate([(up_keep + up_recv).reshape(16, 16, 2048), small_mine], axis=2)

    up_mine, moved, grad_inputs = lax.optimization_barrier((up_mine, moved, grad_inputs))
    down_piece = jnp.sum(moved, axis=0)
    up_piece = jnp.sum(lax.all_to_all(up_mine, PLANE, 0, 0, tiled=True), axis=0)
    down_full = double_z(down_piece)

    up_piece, down_full = lax.optimization_barrier((up_piece, down_full))
    up_full = gather_z(scatter_z(up_piece))
    near = gather_near(jnp.concatenate([down_full, up_full], axis=1))
    own, other = gather_rest(near, gather_sides(near))
    gw_down, gw_up, block = place(own, other)
    return (
        grad_inputs,
        block[:49].reshape(ksize, ksize, channel_count),
        block[51],
        block[49],
        block[50],
        gw_up,
        block[54:58].reshape(-1),
        gw_down,
        block[52],
        block[53],
    )


def solution(mesh):
    fine = Mesh(mesh.devices.reshape(4, 2, 2, 8, 2), AXES)
    image = P(AXES, None, None, None)
    return jax.shard_map(
        body,
        mesh=fine,
        in_specs=(image, image) + (P(),) * 9,
        out_specs=(image,) + (P(),) * 9,
        check_vma=False,
    )
```

```python
import jax
import jax.numpy as jnp
from jax import lax
from jax.experimental import pallas as pl
from jax.experimental.pallas import tpu as pltpu
from jax.sharding import Mesh
from jax.sharding import PartitionSpec as P


AXES = ("y", "xh", "c", "z", "xl")
XAX = ("xh", "xl")
PLANE = ("y", "xh", "xl")
RING4 = [[(i, (i + s) % 4) for i in range(4)] for s in range(4)]
FLIP = [(0, 1), (1, 0)]


def gelu_cdf(pre):
    return 0.5 * (1.0 + lax.erf(pre * 0.7071067811865476))


def gelu_slope(pre):
    cdf = gelu_cdf(pre)
    dens = jnp.exp(-0.5 * pre * pre) * 0.3989422804014327
    return cdf + pre * dens


def coords():
    x = lax.axis_index("xh") * 2 + lax.axis_index("xl")
    return lax.axis_index("c"), x, lax.axis_index("y")


def after(value, *others):
    return lax.optimization_barrier((value,) + others)[0]


def own_half_last(channels):
    c = lax.axis_index("c")
    low, high = channels[:, :256], channels[:, 256:]
    return jnp.where(c == 0, high, low), jnp.where(c == 0, low, high)


def contract(left, right):
    return lax.dot_general(
        left, right, (((0,), (0,)), ((), ())), preferred_element_type=jnp.float32
    )


def sum_z(piece):
    def from_z(v, k):
        return lax.ppermute(v, "z", [(i, i ^ k) for i in range(8)])

    piece = piece + from_z(piece, 1)
    far, near, last = from_z(piece, 4), from_z(piece, 2), from_z(piece, 6)
    return (piece + far) + (near + last)


def gather_near(piece):
    return [
        jnp.concatenate([p] + [lax.ppermute(p, ax, RING4[s]) for s in (1, 2, 3)], axis=0)
        for p, ax in ((piece[:8], "y"), (piece[8:], XAX))
    ]


def gather_sides(near):
    return [
        (lax.ppermute(p, ax, RING4[1]), lax.ppermute(p, ax, RING4[3]))
        for p, ax in zip(near, (XAX, "y"))
    ]


def gather_rest(near, sides):
    out = []
    for p, (below, above), ax in zip(near, sides, (XAX, "y")):
        far = (lax.ppermute(below[:16], ax, RING4[1]), lax.ppermute(above[16:], ax, RING4[3]))
        out += [p, below, above, far[0], far[1]]
    return out, [lax.ppermute(p, "c", FLIP) for p in out]


BLOCKS = ((0, 0, 4), (1, 0, 4), (3, 0, 4), (2, 0, 2), (2, 2, 2))


def place_kernel(far, where, *refs):
    pieces = refs[:10]
    rest, outs, (small, sem) = refs[10:-11], refs[-11:-2], refs[-2:]
    core, x, y = where[0], where[1], where[2]
    copies = []

    def each(part):
        first, second = (x, y) if part == 0 else (y, x)
        for k, (s1, low, count) in enumerate(BLOCKS):
            for s2 in range(low, low + count):
                yield k, lax.rem(first + 4 - s1, 4), lax.rem(second + 4 - s2, 4), (s2 - low) * 8

    half = core if far == 0 else 1 - core
    for part in range(2):
        for k, p1, p2, at in each(part):
            block = p2 * 4 + p1 if part == 0 else p1 * 4 + p2
            src = pieces[part * 5 + k].at[pl.ds(at, 8), :]
            row = pl.multiple_of(half * 256 + block * 16 + part * 8, 8)
            for o in range(2):
                copies.append(
                    pltpu.make_async_copy(
                        src.at[:, pl.ds(o * 2048, 2048)],
                        outs[o].at[pl.ds(row, 8), :],
                        sem.at[len(copies)],
                    )
                )
    for c in copies:
        c.start()
    if far == 1:
        for which, group in ((1 - core, pieces), (core, rest)):
            for k, p1, p2, at in each(0):
                row = pl.multiple_of(which * 32 + p1 * 8, 8)
                lane = pl.multiple_of(p2 * 128, 128)
                small[pl.ds(row, 8), pl.ds(lane, 128)] = group[k][pl.ds(at, 8), pl.ds(4096, 128)]
        for i in range(7):
            outs[2][i] = small[i * 7 : i * 7 + 7, :]
        for i in range(5):
            outs[3 + i][...] = small[49 + i : 50 + i, :]
        for i in range(4):
            outs[8][:, i * 512 : i * 512 + 512] = small[54 + i : 55 + i, :]
    for c in copies:
        c.wait()


def place(own, other):
    c, x, y = coords()
    where = jnp.stack([c, x, y]).astype(jnp.int32)
    vmem = pl.BlockSpec(memory_space=pltpu.VMEM)
    anywhere = pl.BlockSpec(memory_space=pl.ANY)
    large = ((512, 2048),) * 2
    small = ((7, 7, 512),) + ((1, 512),) * 5 + ((1, 2048),)

    def call(far, pieces, whole):
        rest = list(own[:5]) if far else []
        shapes = large + (small if far else ())
        kernel = place_kernel
        if not far:
            kernel = lambda f, *refs: place_kernel(f, *refs[:-4], *refs[-4:-2], *[None] * 7, *refs[-2:])
        return pl.pallas_call(
            lambda *refs: kernel(far, *refs),
            out_shape=tuple(jax.ShapeDtypeStruct(sh, jnp.float32) for sh in shapes),
            in_specs=[pl.BlockSpec(memory_space=pltpu.SMEM)]
            + [vmem] * (10 + len(rest))
            + [anywhere] * len(whole),
            out_specs=(anywhere,) * 2 + (vmem,) * (len(shapes) - 2),
            scratch_shapes=[pltpu.VMEM((64, 512), jnp.float32), pltpu.SemaphoreType.DMA((64,))],
            input_output_aliases={11 + len(rest) + i: i for i in range(len(whole))},
        )(where, *pieces, *rest, *whole)

    return call(1, other, call(0, own, ()))


def forward_kernel(image, kernel, bias, gain, shift, xhat, normed, inv, pad):
    pad[...] = jnp.zeros_like(pad)

    @pl.loop(0, 16)
    def _(h):
        for b in range(4):
            pad[b, h + 3, pl.ds(8, 48), :] = image[h, :, b * 128 : b * 128 + 128].astype(
                jnp.float32
            )

    @pl.loop(0, 4)
    def _(b):
        lanes = pl.ds(pl.multiple_of(b * 128, 128), 128)

        @pl.loop(0, 4)
        def _(group):
            h = group * 4
            acc = [jnp.broadcast_to(bias[:, lanes], (48, 128))] * 4
            for r in range(10):
                for j in range(7):
                    v = pad[b, h + r, pl.ds(5 + j, 48), :]
                    for k in range(4):
                        if 0 <= r - k < 7:
                            acc[k] = acc[k] + v * kernel[r - k, j : j + 1, lanes]
            for k in range(4):
                xhat[pl.ds(pl.multiple_of((h + k) * 48, 48), 48), lanes] = acc[k]

    @pl.loop(0, 16)
    def _(h):
        rows = pl.ds(pl.multiple_of(h * 48, 48), 48)
        mixed = xhat[rows, :]
        mixed = mixed - jnp.mean(mixed, axis=-1, keepdims=True)
        rest = lax.rsqrt(jnp.mean(mixed * mixed, axis=-1, keepdims=True) + 1e-06)
        inv[rows, :] = rest
        unit = mixed * rest
        xhat[rows, :] = unit
        normed[rows, :] = (unit * gain[...] + shift[...]).astype(jnp.bfloat16)


def forward(image, kernel, bias, gain, shift):
    return pl.pallas_call(
        forward_kernel,
        out_shape=(
            jax.ShapeDtypeStruct((768, 512), jnp.float32),
            jax.ShapeDtypeStruct((768, 512), jnp.bfloat16),
            jax.ShapeDtypeStruct((768, 1), jnp.float32),
        ),
        scratch_shapes=[pltpu.VMEM((4, 22, 64, 128), jnp.float32)],
        compiler_params=pltpu.CompilerParams(vmem_limit_bytes=40 << 20),
        name="conv_norm",
    )(image, kernel, bias, gain, shift)


def backward_kernel(gn, xhat, inv, gain, image, upstream, kernel, out, taps, pad, sums, acc):
    pad[...] = jnp.zeros_like(pad)
    sums[...] = jnp.zeros_like(sums)

    def fold(v):
        return jnp.sum(v.reshape(6, 8, 128), axis=0)

    @pl.loop(0, 16)
    def _(h):
        rows = pl.ds(pl.multiple_of(h * 48, 48), 48)
        rest = inv[rows, :]
        gx, xs = [], []
        for b in range(4):
            lanes = slice(b * 128, b * 128 + 128)
            g, x = gn[rows, lanes], xhat[rows, lanes]
            sums[0, :, lanes] += fold(g * x)
            sums[1, :, lanes] += fold(g)
            gx.append(g * gain[:, lanes])
            xs.append(x)
        plain = gx[0] + gx[1] + gx[2] + gx[3]
        cross = gx[0] * xs[0] + gx[1] * xs[1] + gx[2] * xs[2] + gx[3] * xs[3]
        m1 = jnp.sum(plain, axis=-1, keepdims=True) * (1.0 / 512)
        m2 = jnp.sum(cross, axis=-1, keepdims=True) * (1.0 / 512)
        for b in range(4):
            gm = rest * (gx[b] - m1 - xs[b] * m2)
            sums[2, :, b * 128 : b * 128 + 128] += fold(gm)
            pad[b, h + 3, pl.ds(8, 48), :] = gm

    @pl.loop(0, 4)
    def _(b):
        lanes = pl.ds(pl.multiple_of(b * 128, 128), 128)
        acc[...] = jnp.zeros_like(acc)

        @pl.loop(0, 16)
        def _(h):
            x = image[h, :, lanes].astype(jnp.float32)
            back = upstream[h, :, lanes].astype(jnp.float32)
            for i in range(7):
                for j in range(7):
                    t = i * 7 + j
                    g = pad[b, h + 6 - i, pl.ds(11 - j, 48), :]
                    back = back + g * kernel[i, j : j + 1, lanes]
                    acc[t] += fold(g * x)
            out[h, :, lanes] = back.astype(jnp.bfloat16)

        for t in range(49):
            taps[t : t + 1, lanes] = jnp.sum(acc[t], axis=0, keepdims=True) * (1.0 / 256)

    for t in range(3):
        taps[49 + t : 50 + t, :] = jnp.sum(sums[t], axis=0, keepdims=True) * (1.0 / 256)


def backward(gn, xhat, inv, gain, image, upstream, kernel):
    return pl.pallas_call(
        backward_kernel,
        out_shape=(
            jax.ShapeDtypeStruct((16, 48, 512), jnp.bfloat16),
            jax.ShapeDtypeStruct((52, 512), jnp.float32),
        ),
        scratch_shapes=[
            pltpu.VMEM((4, 22, 64, 128), jnp.float32),
            pltpu.VMEM((3, 8, 512), jnp.float32),
            pltpu.VMEM((49, 8, 128), jnp.float32),
        ],
        compiler_params=pltpu.CompilerParams(vmem_limit_bytes=40 << 20),
        cost_estimate=pl.CostEstimate(flops=80000000, bytes_accessed=6000000, transcendentals=0),
        name="conv_back",
    )(gn, xhat, inv, gain, image, upstream, kernel)


def body(
    inputs,
    grad_out,
    conv_kernel,
    conv_bias,
    layer_norm_gain,
    layer_norm_bias,
    w_up,
    up_bias,
    w_down,
    down_bias,
    layer_scale,
):
    image = inputs[0]
    row_count, column_count, channel_count = image.shape
    scale = 1.0 / 256
    gain_row = layer_norm_gain.reshape(1, 512)
    standardized_input, normalized_output, inverse_deviation = forward(
        image, conv_kernel, conv_bias.reshape(1, 512), gain_row, layer_norm_bias.reshape(1, 512)
    )
    pre = jnp.dot(normalized_output, w_up, preferred_element_type=jnp.float32) + up_bias
    hidden = (pre * gelu_cdf(pre)).astype(jnp.bfloat16)
    upstream = grad_out[0].astype(jnp.float32).reshape(row_count * column_count, channel_count)
    g_branch = (upstream * layer_scale).astype(jnp.bfloat16)

    gb_send, gb_keep = own_half_last(g_branch)
    down_send = contract(gb_send, hidden) * scale
    down_keep = contract(gb_keep, hidden) * scale
    down_mine = down_keep + lax.ppermute(down_send, "c", FLIP)

    g_branch_b, pre, _ = lax.optimization_barrier((g_branch, pre, down_send))
    g_hidden = jnp.dot(g_branch_b, w_down, preferred_element_type=jnp.float32)
    g_pre = (g_hidden * gelu_slope(pre)).astype(jnp.bfloat16)

    g_pre, down_mine = lax.optimization_barrier((g_pre, down_mine))
    moved = lax.all_to_all(down_mine.reshape(16, 16, 2048), PLANE, 0, 0, tiled=True)
    norm_send, norm_keep = own_half_last(normalized_output)
    up_send = contract(norm_send, g_pre) * scale
    up_keep = contract(norm_keep, g_pre) * scale
    up_recv = lax.ppermute(up_send, "c", FLIP)

    g_pre_b = after(g_pre, up_keep)
    normalized_gradient = lax.dot_general(
        g_pre_b, w_up, (((1,), (1,)), ((), ())), preferred_element_type=jnp.float32
    )
    grad_inputs, block = backward(
        normalized_gradient,
        standardized_input,
        inverse_deviation,
        gain_row,
        image,
        grad_out[0],
        conv_kernel,
    )
    grad_inputs = grad_inputs.reshape(1, row_count, column_count, channel_count)

    hidden_b, g_pre_c, grad_out_b, g_branch_c, _ = lax.optimization_barrier(
        (hidden, g_pre, grad_out, g_branch, up_keep)
    )
    g_up_bias = jnp.sum(g_pre_c.astype(jnp.float32), axis=0)
    branch = (
        lax.dot_general(
            hidden_b, w_down, (((1,), (1,)), ((), ())), preferred_element_type=jnp.float32
        )
        + down_bias
    )
    g_scale = jnp.sum(grad_out_b.reshape(768, 512).astype(jnp.float32) * branch, axis=0)
    g_down_bias = jnp.sum(g_branch_c.astype(jnp.float32), axis=0)
    rows = jnp.concatenate([g_down_bias, g_scale, g_up_bias]).reshape(6, 512) * scale
    block = jnp.concatenate([block, rows, jnp.zeros((6, 512), jnp.float32)], axis=0)
    c = lax.axis_index("c")
    small_send = jnp.where(c == 0, block[32:], block[:32])
    small_keep = jnp.where(c == 0, block[:32], block[32:])
    small_mine = small_keep + lax.ppermute(small_send, "c", FLIP)
    small_mine = small_mine.reshape(4, 8, 4, 128).transpose(2, 0, 1, 3).reshape(16, 8, 128)
    small_mine = jnp.pad(small_mine, ((0, 0), (0, 8), (0, 0)))
    up_mine = jnp.concatenate([(up_keep + up_recv).reshape(16, 16, 2048), small_mine], axis=2)

    up_mine, moved, grad_inputs = lax.optimization_barrier((up_mine, moved, grad_inputs))
    down_piece = jnp.sum(moved, axis=0)
    up_piece = jnp.sum(lax.all_to_all(up_mine, PLANE, 0, 0, tiled=True), axis=0)
    down_full = sum_z(down_piece)

    up_piece, down_full = lax.optimization_barrier((up_piece, down_full))
    up_full = sum_z(up_piece)
    near = gather_near(jnp.concatenate([down_full, up_full], axis=1))
    own, other = gather_rest(near, gather_sides(near))
    gw_down, gw_up, g_kernel, g_gain, g_shift, g_conv, g_down, g_scale, g_up = place(own, other)
    return (
        grad_inputs,
        g_kernel,
        g_conv.reshape(-1),
        g_gain.reshape(-1),
        g_shift.reshape(-1),
        gw_up,
        g_up.reshape(-1),
        gw_down,
        g_down.reshape(-1),
        g_scale.reshape(-1),
    )


def solution(mesh):
    fine = Mesh(mesh.devices.reshape(4, 2, 2, 8, 2), AXES)
    image = P(AXES, None, None, None)
    return jax.shard_map(
        body,
        mesh=fine,
        in_specs=(image, image) + (P(),) * 9,
        out_specs=(image,) + (P(),) * 9,
        check_vma=False,
    )
```

```python
import jax
import jax.numpy as jnp
from jax import lax
from jax.experimental import pallas as pl
from jax.experimental.pallas import tpu as pltpu
from jax.sharding import Mesh
from jax.sharding import PartitionSpec as P


AXES = ("y", "xh", "c", "z", "xl")
XAX = ("xh", "xl")
PLANE = ("y", "xh", "xl")
RING4 = [[(i, (i + s) % 4) for i in range(4)] for s in range(4)]
FLIP = [(0, 1), (1, 0)]


def gelu_cdf(pre):
    return 0.5 * (1.0 + lax.erf(pre * 0.7071067811865476))


def gelu_slope(pre):
    cdf = gelu_cdf(pre)
    dens = jnp.exp(-0.5 * pre * pre) * 0.3989422804014327
    return cdf + pre * dens


def coords():
    x = lax.axis_index("xh") * 2 + lax.axis_index("xl")
    return lax.axis_index("c"), x, lax.axis_index("y")


def after(value, *others):
    return lax.optimization_barrier((value,) + others)[0]


def own_half_last(channels):
    c = lax.axis_index("c")
    low, high = channels[:, :256], channels[:, 256:]
    return jnp.where(c == 0, high, low), jnp.where(c == 0, low, high)


def contract(left, right):
    return lax.dot_general(
        left, right, (((0,), (0,)), ((), ())), preferred_element_type=jnp.float32
    )


def sum_z(piece):
    def from_z(v, k):
        return lax.ppermute(v, "z", [(i, i ^ k) for i in range(8)])

    piece = piece + from_z(piece, 1)
    far, near, last = from_z(piece, 4), from_z(piece, 2), from_z(piece, 6)
    return (piece + far) + (near + last)


def gather_near(piece):
    return [
        jnp.concatenate([p] + [lax.ppermute(p, ax, RING4[s]) for s in (1, 2, 3)], axis=0)
        for p, ax in ((piece[:8], "y"), (piece[8:], XAX))
    ]


def gather_sides(near):
    return [
        (lax.ppermute(p, ax, RING4[1]), lax.ppermute(p, ax, RING4[3]))
        for p, ax in zip(near, (XAX, "y"))
    ]


def gather_rest(near, sides):
    out = []
    for p, (below, above), ax in zip(near, sides, (XAX, "y")):
        far = (lax.ppermute(below[:16], ax, RING4[1]), lax.ppermute(above[16:], ax, RING4[3]))
        out += [p, below, above, far[0], far[1]]
    return out, [lax.ppermute(p, "c", FLIP) for p in out]


BLOCKS = ((0, 0, 4), (1, 0, 4), (3, 0, 4), (2, 0, 2), (2, 2, 2))


def place_kernel(far, where, *refs):
    pieces = refs[:10]
    rest, outs, (small, sem) = refs[10:-11], refs[-11:-2], refs[-2:]
    core, x, y = where[0], where[1], where[2]
    copies = []

    def each(part):
        first, second = (x, y) if part == 0 else (y, x)
        for k, (s1, low, count) in enumerate(BLOCKS):
            for s2 in range(low, low + count):
                yield k, lax.rem(first + 4 - s1, 4), lax.rem(second + 4 - s2, 4), (s2 - low) * 8

    half = core if far == 0 else 1 - core
    for part in range(2):
        for k, p1, p2, at in each(part):
            block = p2 * 4 + p1 if part == 0 else p1 * 4 + p2
            src = pieces[part * 5 + k].at[pl.ds(at, 8), :]
            row = pl.multiple_of(half * 256 + block * 16 + part * 8, 8)
            for o in range(2):
                copies.append(
                    pltpu.make_async_copy(
                        src.at[:, pl.ds(o * 2048, 2048)],
                        outs[o].at[pl.ds(row, 8), :],
                        sem.at[len(copies)],
                    )
                )
    for c in copies:
        c.start()
    if far == 1:
        for which, group in ((1 - core, pieces), (core, rest)):
            for k, p1, p2, at in each(0):
                row = pl.multiple_of(which * 32 + p1 * 8, 8)
                lane = pl.multiple_of(p2 * 128, 128)
                small[pl.ds(row, 8), pl.ds(lane, 128)] = group[k][pl.ds(at, 8), pl.ds(4096, 128)]
        for i in range(7):
            outs[2][i] = small[i * 7 : i * 7 + 7, :]
        for i in range(5):
            outs[3 + i][...] = small[49 + i : 50 + i, :]
        for i in range(4):
            outs[8][:, i * 512 : i * 512 + 512] = small[54 + i : 55 + i, :]
    for c in copies:
        c.wait()


def place(own, other):
    c, x, y = coords()
    where = jnp.stack([c, x, y]).astype(jnp.int32)
    vmem = pl.BlockSpec(memory_space=pltpu.VMEM)
    anywhere = pl.BlockSpec(memory_space=pl.ANY)
    large = ((512, 2048),) * 2
    small = ((7, 7, 512),) + ((1, 512),) * 5 + ((1, 2048),)

    def call(far, pieces, whole):
        rest = list(own[:5]) if far else []
        shapes = large + (small if far else ())
        kernel = place_kernel
        if not far:
            kernel = lambda f, *refs: place_kernel(f, *refs[:-4], *refs[-4:-2], *[None] * 7, *refs[-2:])
        return pl.pallas_call(
            lambda *refs: kernel(far, *refs),
            out_shape=tuple(jax.ShapeDtypeStruct(sh, jnp.float32) for sh in shapes),
            in_specs=[pl.BlockSpec(memory_space=pltpu.SMEM)]
            + [vmem] * (10 + len(rest))
            + [anywhere] * len(whole),
            out_specs=(anywhere,) * 2 + (vmem,) * (len(shapes) - 2),
            scratch_shapes=[pltpu.VMEM((64, 512), jnp.float32), pltpu.SemaphoreType.DMA((64,))],
            input_output_aliases={11 + len(rest) + i: i for i in range(len(whole))},
        )(where, *pieces, *rest, *whole)

    return call(1, other, call(0, own, ()))


def forward_kernel(image, kernel, bias, gain, shift, xhat, normed, inv, pad):
    pad[...] = jnp.zeros_like(pad)

    @pl.loop(0, 16)
    def _(h):
        for b in range(4):
            pad[b, h + 3, pl.ds(8, 48), :] = image[h, :, b * 128 : b * 128 + 128].astype(
                jnp.float32
            )

    @pl.loop(0, 4)
    def _(b):
        lanes = pl.ds(pl.multiple_of(b * 128, 128), 128)

        @pl.loop(0, 4)
        def _(group):
            h = group * 4
            acc = [jnp.broadcast_to(bias[:, lanes], (48, 128))] * 4
            for r in range(10):
                for j in range(7):
                    v = pad[b, h + r, pl.ds(5 + j, 48), :]
                    for k in range(4):
                        if 0 <= r - k < 7:
                            acc[k] = acc[k] + v * kernel[r - k, j : j + 1, lanes]
            for k in range(4):
                xhat[pl.ds(pl.multiple_of((h + k) * 48, 48), 48), lanes] = acc[k]

    @pl.loop(0, 16)
    def _(h):
        rows = pl.ds(pl.multiple_of(h * 48, 48), 48)
        mixed = xhat[rows, :]
        mixed = mixed - jnp.mean(mixed, axis=-1, keepdims=True)
        rest = lax.rsqrt(jnp.mean(mixed * mixed, axis=-1, keepdims=True) + 1e-06)
        inv[rows, :] = rest
        unit = mixed * rest
        xhat[rows, :] = unit
        normed[rows, :] = (unit * gain[...] + shift[...]).astype(jnp.bfloat16)


def forward(image, kernel, bias, gain, shift):
    return pl.pallas_call(
        forward_kernel,
        out_shape=(
            jax.ShapeDtypeStruct((768, 512), jnp.float32),
            jax.ShapeDtypeStruct((768, 512), jnp.bfloat16),
            jax.ShapeDtypeStruct((768, 1), jnp.float32),
        ),
        scratch_shapes=[pltpu.VMEM((4, 22, 64, 128), jnp.float32)],
        compiler_params=pltpu.CompilerParams(vmem_limit_bytes=40 << 20),
        name="conv_norm",
    )(image, kernel, bias, gain, shift)


def backward_kernel(gn, xhat, inv, gain, image, pad, taps, sums, acc):
    pad[...] = jnp.zeros_like(pad)
    sums[...] = jnp.zeros_like(sums)

    def fold(v):
        return jnp.sum(v.reshape(6, 8, 128), axis=0)

    @pl.loop(0, 16)
    def _(h):
        rows = pl.ds(pl.multiple_of(h * 48, 48), 48)
        rest = inv[rows, :]
        gx, xs = [], []
        for b in range(4):
            lanes = slice(b * 128, b * 128 + 128)
            g, x = gn[rows, lanes], xhat[rows, lanes]
            sums[0, :, lanes] += fold(g * x)
            sums[1, :, lanes] += fold(g)
            gx.append(g * gain[:, lanes])
            xs.append(x)
        plain = gx[0] + gx[1] + gx[2] + gx[3]
        cross = gx[0] * xs[0] + gx[1] * xs[1] + gx[2] * xs[2] + gx[3] * xs[3]
        m1 = jnp.sum(plain, axis=-1, keepdims=True) * (1.0 / 512)
        m2 = jnp.sum(cross, axis=-1, keepdims=True) * (1.0 / 512)
        for b in range(4):
            gm = rest * (gx[b] - m1 - xs[b] * m2)
            sums[2, :, b * 128 : b * 128 + 128] += fold(gm)
            pad[b, h + 3, pl.ds(8, 48), :] = gm

    @pl.loop(0, 4)
    def _(b):
        lanes = pl.ds(pl.multiple_of(b * 128, 128), 128)
        acc[...] = jnp.zeros_like(acc)

        @pl.loop(0, 8)
        def _(pair):
            h = pair * 2
            x = [image[h + k, :, lanes].astype(jnp.float32) for k in range(2)]
            for r in range(8):
                for j in range(7):
                    g = pad[b, h + r, pl.ds(11 - j, 48), :]
                    for k in range(2):
                        i = 6 + k - r
                        if 0 <= i < 7:
                            acc[i * 7 + j] += fold(g * x[k])

        for t in range(49):
            taps[t : t + 1, lanes] = jnp.sum(acc[t], axis=0, keepdims=True) * (1.0 / 256)

    for t in range(3):
        taps[49 + t : 50 + t, :] = jnp.sum(sums[t], axis=0, keepdims=True) * (1.0 / 256)


def backward(gn, xhat, inv, gain, image):
    return pl.pallas_call(
        backward_kernel,
        out_shape=(
            jax.ShapeDtypeStruct((4, 22, 64, 128), jnp.float32),
            jax.ShapeDtypeStruct((52, 512), jnp.float32),
        ),
        scratch_shapes=[
            pltpu.VMEM((3, 8, 512), jnp.float32),
            pltpu.VMEM((49, 8, 128), jnp.float32),
        ],
        compiler_params=pltpu.CompilerParams(vmem_limit_bytes=40 << 20),
        cost_estimate=pl.CostEstimate(flops=40000000, bytes_accessed=6000000, transcendentals=0),
        name="norm_back",
    )(gn, xhat, inv, gain, image)


def spread_kernel(pad, upstream, kernel, out):
    @pl.loop(0, 4)
    def _(b):
        lanes = pl.ds(pl.multiple_of(b * 128, 128), 128)

        @pl.loop(0, 4)
        def _(group):
            h = group * 4
            back = [upstream[h + k, :, lanes].astype(jnp.float32) for k in range(4)]
            for r in range(10):
                for j in range(7):
                    g = pad[b, h + r, pl.ds(11 - j, 48), :]
                    for k in range(4):
                        i = 6 + k - r
                        if 0 <= i < 7:
                            back[k] = back[k] + g * kernel[i, j : j + 1, lanes]
            for k in range(4):
                out[h + k, :, lanes] = back[k].astype(jnp.bfloat16)


def spread(pad, upstream, kernel):
    return pl.pallas_call(
        spread_kernel,
        out_shape=jax.ShapeDtypeStruct((16, 48, 512), jnp.bfloat16),
        compiler_params=pltpu.CompilerParams(vmem_limit_bytes=16 << 20),
        cost_estimate=pl.CostEstimate(flops=40000000, bytes_accessed=6000000, transcendentals=0),
        name="conv_back",
    )(pad, upstream, kernel)


def body(
    inputs,
    grad_out,
    conv_kernel,
    conv_bias,
    layer_norm_gain,
    layer_norm_bias,
    w_up,
    up_bias,
    w_down,
    down_bias,
    layer_scale,
):
    image = inputs[0]
    row_count, column_count, channel_count = image.shape
    scale = 1.0 / 256
    gain_row = layer_norm_gain.reshape(1, 512)
    standardized_input, normalized_output, inverse_deviation = forward(
        image, conv_kernel, conv_bias.reshape(1, 512), gain_row, layer_norm_bias.reshape(1, 512)
    )
    pre = jnp.dot(normalized_output, w_up, preferred_element_type=jnp.float32) + up_bias
    hidden = (pre * gelu_cdf(pre)).astype(jnp.bfloat16)
    upstream = grad_out[0].astype(jnp.float32).reshape(row_count * column_count, channel_count)
    g_branch = (upstream * layer_scale).astype(jnp.bfloat16)

    gb_send, gb_keep = own_half_last(g_branch)
    down_send = contract(gb_send, hidden) * scale
    down_keep = contract(gb_keep, hidden) * scale
    down_recv = lax.ppermute(down_send, "c", FLIP)
    down_keep, down_recv = lax.optimization_barrier((down_keep, down_recv))
    down_mine = down_keep + down_recv

    g_branch_b, pre, _ = lax.optimization_barrier((g_branch, pre, down_send))

    down_mine, g_branch_b, pre = lax.optimization_barrier((down_mine, g_branch_b, pre))
    moved = lax.all_to_all(down_mine.reshape(16, 16, 2048), PLANE, 0, 0, tiled=True)
    g_hidden = jnp.dot(g_branch_b, w_down, preferred_element_type=jnp.float32)
    g_pre = (g_hidden * gelu_slope(pre)).astype(jnp.bfloat16)
    norm_send, norm_keep = own_half_last(normalized_output)
    up_send = contract(norm_send, g_pre) * scale
    up_keep = contract(norm_keep, g_pre) * scale
    up_recv = lax.ppermute(up_send, "c", FLIP)

    g_pre_b = after(g_pre, up_keep)
    normalized_gradient = lax.dot_general(
        g_pre_b, w_up, (((1,), (1,)), ((), ())), preferred_element_type=jnp.float32
    )
    g_mixed, block = backward(
        normalized_gradient, standardized_input, inverse_deviation, gain_row, image
    )

    hidden_b, g_pre_c, grad_out_b, g_branch_c, _ = lax.optimization_barrier(
        (hidden, g_pre, grad_out, g_branch, up_keep)
    )
    g_up_bias = jnp.sum(g_pre_c.astype(jnp.float32), axis=0)
    branch = (
        lax.dot_general(
            hidden_b, w_down, (((1,), (1,)), ((), ())), preferred_element_type=jnp.float32
        )
        + down_bias
    )
    g_scale = jnp.sum(grad_out_b.reshape(768, 512).astype(jnp.float32) * branch, axis=0)
    g_down_bias = jnp.sum(g_branch_c.astype(jnp.float32), axis=0)
    rows = jnp.concatenate([g_down_bias, g_scale, g_up_bias]).reshape(6, 512) * scale
    block = jnp.concatenate([block, rows, jnp.zeros((6, 512), jnp.float32)], axis=0)
    c = lax.axis_index("c")
    small_send = jnp.where(c == 0, block[32:], block[:32])
    small_keep = jnp.where(c == 0, block[:32], block[32:])
    small_mine = small_keep + lax.ppermute(small_send, "c", FLIP)
    small_mine = small_mine.reshape(4, 8, 4, 128).transpose(2, 0, 1, 3).reshape(16, 8, 128)
    up_keep, up_recv, small_mine = lax.optimization_barrier((up_keep, up_recv, small_mine))
    up_mine = jnp.pad((up_keep + up_recv).reshape(16, 16, 2048), ((0, 0), (0, 0), (0, 128)))
    up_mine = lax.dynamic_update_slice(up_mine, small_mine, (0, 0, 2048))

    up_mine, moved, g_mixed = lax.optimization_barrier((up_mine, moved, g_mixed))
    down_piece = jnp.sum(moved, axis=0)
    up_moved = lax.all_to_all(up_mine, PLANE, 0, 0, tiled=True)
    up_piece = jnp.sum(up_moved, axis=0)
    grad_inputs = spread(g_mixed, grad_out[0], conv_kernel)
    grad_inputs = grad_inputs.reshape(1, row_count, column_count, channel_count)
    down_full = sum_z(down_piece)

    up_piece, down_full = lax.optimization_barrier((up_piece, down_full))
    up_full = sum_z(up_piece)
    near = gather_near(jnp.concatenate([down_full, up_full], axis=1))
    own, other = gather_rest(near, gather_sides(near))
    gw_down, gw_up, g_kernel, g_gain, g_shift, g_conv, g_down, g_scale, g_up = place(own, other)
    return (
        grad_inputs,
        g_kernel,
        g_conv.reshape(-1),
        g_gain.reshape(-1),
        g_shift.reshape(-1),
        gw_up,
        g_up.reshape(-1),
        gw_down,
        g_down.reshape(-1),
        g_scale.reshape(-1),
    )


def solution(mesh):
    fine = Mesh(mesh.devices.reshape(4, 2, 2, 8, 2), AXES)
    image = P(AXES, None, None, None)
    return jax.shard_map(
        body,
        mesh=fine,
        in_specs=(image, image) + (P(),) * 9,
        out_specs=(image,) + (P(),) * 9,
        check_vma=False,
    )
```
